32 devices in a mesh: grp: 2 (over x), tile: 8 (over z, y), mem: 2 (over core).
Axes of the slice: x: 2, y: 2, z: 4, core: 2. Of those that a mesh axis runs over, the one named last changes fastest.
Arguments:
- increment: float32 [64, 512, 512], P('grp', 'tile'), parts along dimension 0, may hold values from -6 to 6
- perturbations: bfloat16 [24, 64, 512, 512], P('mem', 'grp', 'tile'), parts along dimension 1, may hold values from -3 to 3
- localization: bfloat16 [18, 256, 256], replicated, may hold values from -1 to 3, as said below
Outputs:
- covariance_product: float32 [64, 512, 512], P('grp', 'tile', 'mem'), parts along dimension 0
The draws below stay inside these ranges and needn't reach their ends.
There are 2 independent parts, one for each index of `grp`. The reference program is written for one: setup_inputs(seed, part) draws one part's arguments, and reference() takes and returns one part's arrays. A program takes and returns all parts, laid end to end along the dimension named above; an argument that names none is the same for every part. Nothing has to cross between parts.
Inputs may be any that keep to these rules, and one draw needn't show every extreme that they name: mode-dependent localization matrices.
All inputs are finite; a program needn't handle non-finite values.
Results may differ from the reference program's by a relative error of at most 0.0052.
Values may be sent and summed in bfloat16 or wider, within the bound.
No kernel may reach another device: no remote copies, remote signals or barrier semaphores. Data moves between devices by JAX's collectives and lax.ppermute only.
A program may use at most 128 MiB of HBM per device.

```python
import math
import jax
import jax.numpy as jnp
from jax import lax

NX = 512
NY = 512
NZ = 32
MX = 256
MY = 256
MZ = 18
MEMBERS = 24


def draw_localization(key, part):
    first_key, second_key = jax.random.split(jax.random.fold_in(key, 7))
    rough = jax.random.normal(first_key, (MZ, MX, MX), jnp.float32)
    diagonal = jnp.exp(jax.random.uniform(second_key, (MZ, MX), jnp.float32, math.log(0.5), math.log(2.0)))
    identity_matrix = jnp.eye(MX, dtype=jnp.float32)
    rough = jnp.clip(rough, -6.0, 6.0)
    return (identity_matrix[None] * diagonal[:, None, :] + 0.5 * rough / math.sqrt(MX)).astype(jnp.bfloat16)


def block_levels(rng, extent, pieces, least, high):
    def one(axis_at, shards_of):
        steps = jax.random.uniform(jax.random.fold_in(jax.random.fold_in(rng, 6), axis_at), (shards_of,), jnp.float32, least / len(pieces), high / len(pieces))
        return jnp.repeat(jnp.exp(steps), extent[axis_at] // shards_of).reshape((-1,) + (1,) * (len(extent) - axis_at - 1))

    level = one(*pieces[0])
    for cut in pieces[1:]:
        level = level * one(*cut)
    return level


def centred(stream_key, dims, width, bound, cuts=(), kind=jnp.bfloat16):
    array = width * jax.random.normal(stream_key, dims, jnp.float32)
    if cuts:
        array = array * block_levels(stream_key, dims, cuts, -0.22, 0.18)
    return jnp.clip(array, -bound, bound).astype(kind)


def setup_inputs(seed: int = 0, part: int = 0) -> dict:
    keys = jax.random.split(jax.random.key(seed), 4)
    part_splits = jax.random.split(jax.random.fold_in(keys[3], part), 4)
    return {
        "increment": centred(part_splits[0], (NZ, NX, NY), 1.0, 6.0, ((1, 8),), jnp.float32),
        "perturbations": centred(part_splits[1], (MEMBERS, NZ, NX, NY), 0.5, 3.0, ((0, 2), (2, 8))),
        "localization": draw_localization(jax.random.fold_in(keys[3], 71), part),
    }


def make_table(modes, cells):
    index = jnp.arange(modes, dtype=jnp.float32)[:, None]
    points = jnp.arange(cells, dtype=jnp.float32)[None, :]
    weights = jnp.where(index == 0, math.sqrt(1.0 / cells), math.sqrt(2.0 / cells))
    return (weights * jnp.cos(math.pi * index * (2.0 * points + 1.0) / (2.0 * cells))).astype(jnp.bfloat16)

def reference(increment, perturbations, localization):
    table_y = make_table(MY, NY).astype(jnp.float32)
    table_z = make_table(MZ, NZ).astype(jnp.float32)
    table_x = make_table(MX, NX).astype(jnp.float32)
    localization_matrices = localization.astype(jnp.float32)

    def member_index(summed, pert):
        wide = pert.astype(jnp.float32)
        product = (wide * increment).astype(jnp.bfloat16).astype(jnp.float32)
        along_y = jnp.einsum('zxn,yn->zxy', product, table_y).astype(jnp.bfloat16).astype(jnp.float32)
        along_z = jnp.einsum('cz,zxy->cxy', table_z, along_y).astype(jnp.bfloat16).astype(jnp.float32)
        spectral_weights = jnp.einsum('cxy,kx->cyk', along_z, table_x).astype(jnp.bfloat16).astype(jnp.float32)
        localized_field = jnp.einsum('fnx,fox->fno', spectral_weights, localization_matrices).astype(jnp.bfloat16).astype(jnp.float32)
        back_x = jnp.einsum('cyl,lx->cxy', localized_field, table_x).astype(jnp.bfloat16).astype(jnp.float32)
        back_z = jnp.einsum('cxy,cz->zxy', back_x, table_z).astype(jnp.bfloat16).astype(jnp.float32)
        back_y = jnp.einsum('zxy,yn->zxn', back_z, table_y)
        return (summed + wide * back_y, None)
    summed, unused = lax.scan(member_index, jnp.zeros((NZ, NX, NY), jnp.float32), perturbations)
    return summed
```

```python
import math

import jax
import jax.numpy as jnp
import numpy as np
from jax import lax
from jax.experimental import pallas as pl
from jax.experimental.pallas import tpu as pltpu
from jax.sharding import PartitionSpec as P

MY = 256
LANES = 128
ROWS = 16
HALF = 8


def make_table(modes, cells):
    index = np.arange(modes, dtype=np.float32)[:, None]
    points = np.arange(cells, dtype=np.float32)[None, :]
    weights = np.where(index == 0, math.sqrt(1.0 / cells), math.sqrt(2.0 / cells))
    angles = np.float32(math.pi) * index * (2.0 * points + 1.0) / np.float32(2.0 * cells)
    return (weights.astype(np.float32) * np.cos(angles)).astype(jnp.bfloat16)


def dot(a, b):
    return jnp.dot(a, b, preferred_element_type=jnp.float32)


def restrict_kernel(tiles, width, ids, pert, inc, table, vertical, *rest):
    outs, stage = rest[:tiles], rest[tiles]
    count, levels = pert.shape[0], pert.shape[1]
    halves = ROWS // HALF
    modes = vertical.shape[0] // HALF
    lane_blocks = table.shape[1] // LANES
    first = pl.program_id(1) * count
    field = inc[...]
    for m in range(count):
        product = (pert[m].astype(jnp.float32) * field).astype(jnp.bfloat16)
        along_y = dot(product.reshape(levels * ROWS, -1), table[...])
        along_y = along_y.reshape(levels, halves, HALF, -1)
        parts = []
        for h in range(halves):
            part = along_y[:, h].reshape(levels * HALF, -1).astype(jnp.bfloat16)
            parts.append(dot(vertical[...], part).reshape(modes, HALF, -1))
        along_z = jnp.concatenate(parts, axis=1).astype(jnp.bfloat16)
        for c in range(modes):
            for q in range(lane_blocks):
                stage[(c * width + first + m) * lane_blocks + q] = along_z[
                    c, :, q * LANES : (q + 1) * LANES
                ]

    @pl.when(pl.program_id(1) == pl.num_programs(1) - 1)
    def _():
        units = outs[0].shape[0]
        for s in range(tiles):
            outs[s][...] = stage[pl.ds(jnp.bitwise_xor(ids[0], s) * units, units)]


def localize_kernel(tiles, group, ids, *rest):
    pieces, rest = rest[:tiles], rest[tiles:]
    matrices, rest = rest[:group], rest[group:]
    table, table_t = rest[:2]
    outs, field, prolonged = rest[2 : 2 + tiles], rest[2 + tiles], rest[3 + tiles]
    height = pieces[0].shape[1]
    for s in range(tiles):
        base = pl.multiple_of(jnp.bitwise_xor(ids[0], s) * height, height)
        for g in range(group):
            field[pl.ds(base, height), g * LANES : (g + 1) * LANES] = pieces[s][g]
    spectral = dot(table[...], field[...]).astype(jnp.bfloat16)
    localized = [
        dot(matrices[g][0], spectral[:, g * LANES : (g + 1) * LANES]).astype(jnp.bfloat16)
        for g in range(group)
    ]
    prolonged[...] = dot(table_t[...], jnp.concatenate(localized, axis=1)).astype(jnp.bfloat16)
    for s in range(tiles):
        base = pl.multiple_of(jnp.bitwise_xor(ids[0], s) * height, height)
        for g in range(group):
            outs[s][g] = prolonged[pl.ds(base, height), g * LANES : (g + 1) * LANES]


def prolong_kernel(tiles, width, start, final, ids, pert, table, vertical, *rest):
    pieces, rest = rest[:tiles], rest[tiles:]
    before, rest = (None, rest) if start else (rest[0], rest[1:])
    outs, (stage, total) = rest[:-2], rest[-2:]
    count, levels = pert.shape[0], pert.shape[1]
    halves = ROWS // HALF
    modes = vertical.shape[1] // HALF
    lane_blocks = table.shape[0] // LANES
    first = pl.program_id(1) * count

    @pl.when(pl.program_id(1) == 0)
    def _():
        units = pieces[0].shape[0]
        for s in range(tiles):
            stage[pl.ds(jnp.bitwise_xor(ids[0], s) * units, units)] = pieces[s][...]
        total[...] = jnp.zeros_like(total) if start else before[...]

    for m in range(count):
        rows = []
        for c in range(modes):
            unit = (c * width + first + m) * lane_blocks
            rows.append(
                jnp.concatenate([stage[unit + q] for q in range(lane_blocks)], axis=1)
            )
        back_x = jnp.stack(rows).astype(jnp.float32).reshape(modes, halves, HALF, -1)
        for h in range(halves):
            part = back_x[:, h].reshape(modes * HALF, -1).astype(jnp.bfloat16)
            back_z = dot(vertical[...], part).astype(jnp.bfloat16)
            back_y = dot(back_z, table[...]).reshape(levels, HALF, -1)
            wide = pert[m].astype(jnp.float32)[:, h * HALF : (h + 1) * HALF]
            total[:, h * HALF : (h + 1) * HALF] += wide * back_y

    @pl.when(pl.program_id(1) == pl.num_programs(1) - 1)
    def _():
        if final:
            own, other = outs
            half = own.shape[2]
            own[...] = total[:, :, pl.ds(pl.multiple_of(ids[1] * half, half), half)]
            other[...] = total[:, :, pl.ds(pl.multiple_of((1 - ids[1]) * half, half), half)]
        else:
            outs[0][...] = total[...]


def chunk_plan(members, units_per_member, tiles):
    base = next(
        b
        for b in range(1, members + 1)
        if members % b == 0 and (b * units_per_member) % tiles == 0
    )
    left = members // base
    plan = []
    if left >= 4:
        plan, left = [1], left - 2
        while left >= 2:
            plan, left = plan + [2], left - 2
        plan = plan + [1] * left + [1]
    else:
        plan = [1] * left
    return base, plan


def solution(mesh):
    tiles = mesh.shape["tile"]
    VMEM_LIMIT = 30 * 1024 * 1024

    def call(kernel, flops, moved, **kwargs):
        return pl.pallas_call(
            kernel,
            compiler_params=pltpu.CompilerParams(vmem_limit_bytes=VMEM_LIMIT),
            cost_estimate=pl.CostEstimate(
                flops=int(flops), bytes_accessed=int(moved), transcendentals=0
            ),
            **kwargs,
        )

    def shards(increment, perturbations, localization):
        members, levels, height, columns = perturbations.shape
        modes, modes_x, _ = localization.shape
        lane_blocks = MY // LANES
        table_y = make_table(MY, columns)
        table_x = make_table(modes_x, height * tiles)
        table_z = make_table(modes, levels)
        eye = np.eye(HALF, dtype=np.float32)
        vertical = np.kron(table_z.astype(np.float32), eye).astype(jnp.bfloat16)
        y_in, y_out = jnp.asarray(table_y.T), jnp.asarray(table_y)
        x_in, x_out = jnp.asarray(table_x), jnp.asarray(table_x.T)
        z_in, z_out = jnp.asarray(vertical), jnp.asarray(vertical.T)
        ids = jnp.stack([lax.axis_index("tile"), lax.axis_index("mem")]).astype(jnp.int32)
        blocks = height // ROWS
        base, plan = chunk_plan(members, modes * lane_blocks, tiles)
        whole = lambda a: pl.BlockSpec(a.shape, lambda *_: (0,) * a.ndim)

        def pert_spec(offset):
            return pl.BlockSpec(
                (base, levels, ROWS, columns), lambda x, m, _: (offset + m, 0, x, 0)
            )

        def exchange(pieces):
            moved = [pieces[0]]
            for s in range(1, tiles):
                pairs = [(k, k ^ s) for k in range(tiles)]
                moved.append(lax.ppermute(pieces[s], "tile", pairs))
            return moved

        def restrict(offset, steps):
            width = steps * base
            units = width * modes * lane_blocks // tiles
            piece = jax.ShapeDtypeStruct((units, height, LANES), jnp.bfloat16)
            pixels = width * height
            return call(
                lambda *refs: restrict_kernel(tiles, width, *refs),
                flops=2 * pixels * levels * MY * (columns + modes * HALF),
                moved=2 * pixels * levels * columns + 4 * increment.size,
                out_shape=[piece] * tiles,
                grid_spec=pltpu.PrefetchScalarGridSpec(
                    num_scalar_prefetch=1,
                    grid=(blocks, steps),
                    in_specs=[
                        pert_spec(offset),
                        pl.BlockSpec((levels, ROWS, columns), lambda x, m, _: (0, x, 0)),
                        whole(y_in),
                        whole(z_in),
                    ],
                    out_specs=[pl.BlockSpec((units, ROWS, LANES), lambda x, m, _: (0, x, 0))]
                    * tiles,
                    scratch_shapes=[pltpu.VMEM((units * tiles, ROWS, LANES), jnp.bfloat16)],
                ),
            )(ids, perturbations, increment, y_in, z_in)

        def localize(pieces, steps):
            width = steps * base
            units = pieces[0].shape[0]
            group = next(g for g in (3, 2, 1) if units % g == 0)
            spec = pl.BlockSpec((group, height, LANES), lambda i, _: (i, 0, 0))

            def matrix_spec(g):
                def index(i, ids):
                    return ((ids[0] * units + i * group + g) // (width * lane_blocks), 0, 0)

                return pl.BlockSpec((1, modes_x, modes_x), index)

            cells = height * tiles
            wide = group * LANES
            return call(
                lambda *refs: localize_kernel(tiles, group, *refs),
                flops=2 * units * LANES * modes_x * (2 * cells + modes_x),
                moved=units * (4 * LANES * cells + 2 * modes_x * modes_x),
                out_shape=[jax.ShapeDtypeStruct(pieces[0].shape, jnp.bfloat16)] * tiles,
                grid_spec=pltpu.PrefetchScalarGridSpec(
                    num_scalar_prefetch=1,
                    grid=(units // group,),
                    in_specs=[spec] * tiles
                    + [matrix_spec(g) for g in range(group)]
                    + [whole(x_in), whole(x_out)],
                    out_specs=[spec] * tiles,
                    scratch_shapes=[
                        pltpu.VMEM((cells, wide), jnp.bfloat16),
                        pltpu.VMEM((cells, wide), jnp.bfloat16),
                    ],
                ),
            )(ids, *pieces, *([localization] * group), x_in, x_out)

        def prolong(pieces, before, offset, steps, final):
            width = steps * base
            units = pieces[0].shape[0]
            full = jax.ShapeDtypeStruct(increment.shape, jnp.float32)
            part = jax.ShapeDtypeStruct((levels, height, columns // 2), jnp.float32)
            block = lambda n: pl.BlockSpec((levels, ROWS, n), lambda x, m, _: (0, x, 0))
            start = before is None
            pixels = width * height
            return call(
                lambda *refs: prolong_kernel(tiles, width, start, final, *refs),
                flops=2 * pixels * levels * MY * (columns + modes * HALF),
                moved=2 * pixels * levels * columns + 8 * increment.size,
                out_shape=[part, part] if final else [full],
                grid_spec=pltpu.PrefetchScalarGridSpec(
                    num_scalar_prefetch=1,
                    grid=(blocks, steps),
                    in_specs=[pert_spec(offset), whole(y_out), whole(z_out)]
                    + [pl.BlockSpec((units, ROWS, LANES), lambda x, m, _: (0, x, 0))] * tiles
                    + ([] if start else [block(columns)]),
                    out_specs=[block(columns // 2)] * 2 if final else [block(columns)],
                    scratch_shapes=[
                        pltpu.VMEM((units * tiles, ROWS, LANES), jnp.bfloat16),
                        pltpu.VMEM((levels, ROWS, columns), jnp.float32),
                    ],
                ),
            )(ids, perturbations, y_out, z_out, *pieces, *([] if start else [before]))

        offsets = [sum(plan[:i]) for i in range(len(plan))]
        arrived = [exchange(restrict(o, n)) for o, n in zip(offsets, plan)]
        returned = [exchange(localize(p, n)) for p, n in zip(arrived, plan)]
        total = None
        for i, (o, n) in enumerate(zip(offsets, plan)):
            final = i == len(plan) - 1
            result = prolong(returned[i], total, o, n, final)
            total = None if final else result[0]
        own, other = result
        return own + lax.ppermute(other, "mem", [(0, 1), (1, 0)])

    return jax.shard_map(
        shards,
        mesh=mesh,
        in_specs=(P("grp", "tile", None), P("mem", "grp", "tile", None), P()),
        out_specs=P("grp", "tile", "mem"),
        check_vma=False,
    )
```

```python
import functools
import math

import jax
import jax.numpy as jnp
import numpy as np
from jax import lax
from jax.experimental import pallas as pl
from jax.experimental.pallas import tpu as pltpu
from jax.sharding import PartitionSpec as P


MY = 256
LANES = 128
ROWS = 16
HALF = 8


def make_table(modes, cells):
    index = np.arange(modes, dtype=np.float32)[:, None]
    points = np.arange(cells, dtype=np.float32)[None, :]
    weights = np.where(index == 0, math.sqrt(1.0 / cells), math.sqrt(2.0 / cells))
    angles = np.float32(math.pi) * index * (2.0 * points + 1.0) / np.float32(2.0 * cells)
    return (weights.astype(np.float32) * np.cos(angles)).astype(jnp.bfloat16)


def partners(tiles):
    order = [0]
    for s in range(tiles // 2):
        order += [tiles // 2 + s, s + 1]
    return order[:tiles]


def dot(a, b):
    return jnp.dot(a, b, preferred_element_type=jnp.float32)


def restrict_kernel(tiles, width, ids, pert, inc, table, vertical, *rest):
    outs, stage = rest[:tiles], rest[tiles]
    count, levels = pert.shape[0], pert.shape[1]
    halves = ROWS // HALF
    modes = vertical.shape[0] // HALF
    lane_blocks = table.shape[1] // LANES
    first = pl.program_id(1) * count
    field = inc[...]
    for m in range(count):
        product = (pert[m].astype(jnp.float32) * field).astype(jnp.bfloat16)
        along_y = dot(product.reshape(levels * ROWS, -1), table[...])
        along_y = along_y.reshape(levels, halves, HALF, -1)
        parts = []
        for h in range(halves):
            part = along_y[:, h].reshape(levels * HALF, -1).astype(jnp.bfloat16)
            parts.append(dot(vertical[...], part).reshape(modes, HALF, -1))
        along_z = jnp.concatenate(parts, axis=1).astype(jnp.bfloat16)
        for c in range(modes):
            for q in range(lane_blocks):
                stage[(c * width + first + m) * lane_blocks + q] = along_z[
                    c, :, q * LANES : (q + 1) * LANES
                ]

    @pl.when(pl.program_id(1) == pl.num_programs(1) - 1)
    def _():
        units = outs[0].shape[0]
        for out, s in zip(outs, partners(tiles)):
            out[...] = stage[pl.ds(jnp.bitwise_xor(ids[0], s) * units, units)]


def localize_kernel(tiles, group, cuts, ids, *rest):
    pieces, rest = rest[: tiles * cuts], rest[tiles * cuts :]
    matrices, rest = rest[:group], rest[group:]
    table, table_t = rest[:2]
    outs, (field, prolonged) = rest[2:-2], rest[-2:]
    height = field.shape[0] // tiles
    order = partners(tiles)

    def places(refs):
        start = 0
        for i, ref in enumerate(refs):
            base = jnp.bitwise_xor(ids[0], order[i % tiles]) * height + start
            yield ref, pl.ds(pl.multiple_of(base, ROWS), ref.shape[1])
            start += ref.shape[1] if i % tiles == tiles - 1 else 0

    for piece, rows in places(pieces):
        for g in range(group):
            field[rows, g * LANES : (g + 1) * LANES] = piece[g]
    spectral = dot(table[...], field[...]).astype(jnp.bfloat16)
    localized = [
        dot(matrices[g][0], spectral[:, g * LANES : (g + 1) * LANES]).astype(jnp.bfloat16)
        for g in range(group)
    ]
    prolonged[...] = dot(table_t[...], jnp.concatenate(localized, axis=1)).astype(jnp.bfloat16)
    for out, rows in places(outs):
        for g in range(group):
            out[g] = prolonged[rows, g * LANES : (g + 1) * LANES]


def prolong_kernel(tiles, width, start, final, ids, pert, table, vertical, *rest):
    pieces, rest = rest[:tiles], rest[tiles:]
    before, rest = (None, rest) if start else (rest[0], rest[1:])
    outs, (stage, total) = rest[:-2], rest[-2:]
    count, levels = pert.shape[0], pert.shape[1]
    halves = ROWS // HALF
    modes = vertical.shape[1] // HALF
    lane_blocks = table.shape[0] // LANES
    first = pl.program_id(1) * count

    @pl.when(pl.program_id(1) == 0)
    def _():
        units = pieces[0].shape[0]
        for piece, s in zip(pieces, partners(tiles)):
            stage[pl.ds(jnp.bitwise_xor(ids[0], s) * units, units)] = piece[...]
        total[...] = jnp.zeros_like(total) if start else before[...]

    for m in range(count):
        rows = []
        for c in range(modes):
            unit = (c * width + first + m) * lane_blocks
            rows.append(
                jnp.concatenate([stage[unit + q] for q in range(lane_blocks)], axis=1)
            )
        back_x = jnp.stack(rows).astype(jnp.float32).reshape(modes, halves, HALF, -1)
        for h in range(halves):
            part = back_x[:, h].reshape(modes * HALF, -1).astype(jnp.bfloat16)
            back_z = dot(vertical[...], part).astype(jnp.bfloat16)
            back_y = dot(back_z, table[...]).reshape(levels, HALF, -1)
            wide = pert[m].astype(jnp.float32)[:, h * HALF : (h + 1) * HALF]
            total[:, h * HALF : (h + 1) * HALF] += wide * back_y

    @pl.when(pl.program_id(1) == pl.num_programs(1) - 1)
    def _():
        if final:
            own, other = outs
            half = own.shape[2]
            own[...] = total[:, :, pl.ds(pl.multiple_of(ids[1] * half, half), half)]
            other[...] = total[:, :, pl.ds(pl.multiple_of((1 - ids[1]) * half, half), half)]
        else:
            outs[0][...] = total[...]


def finish_kernel(*refs):
    own, received, out = refs[0], refs[1], refs[-1]
    out[...] = own[...] + received[...]


def chunk_plan(members, units_per_member, tiles):
    base = next(
        b
        for b in range(1, members + 1)
        if members % b == 0 and (b * units_per_member) % tiles == 0
    )
    left = members // base
    plan = []
    if left >= 5:
        plan, left = [1, 1], left - 4
        while left >= 2:
            plan, left = plan + [2], left - 2
        plan = plan + [1] * left + [1, 1]
    else:
        plan = [1] * left
    return base, plan


def solution(mesh):
    tiles = mesh.shape["tile"]

    def call(kernel, flops, moved, grant=30, **kwargs):
        return pl.pallas_call(
            kernel,
            compiler_params=pltpu.CompilerParams(vmem_limit_bytes=grant * 1024 * 1024),
            cost_estimate=pl.CostEstimate(
                flops=int(flops), bytes_accessed=int(moved), transcendentals=0
            ),
            **kwargs,
        )

    def shards(increment, perturbations, localization, base, plan, heads, tails):
        _, levels, height, columns = perturbations.shape
        modes, modes_x, _ = localization.shape
        lane_blocks = MY // LANES
        table_y = make_table(MY, columns)
        table_x = make_table(modes_x, height * tiles)
        table_z = make_table(modes, levels)
        eye = np.eye(HALF, dtype=np.float32)
        vertical = np.kron(table_z.astype(np.float32), eye).astype(jnp.bfloat16)
        y_in, y_out = jnp.asarray(table_y.T), jnp.asarray(table_y)
        x_in, x_out = jnp.asarray(table_x), jnp.asarray(table_x.T)
        z_in, z_out = jnp.asarray(vertical), jnp.asarray(vertical.T)
        ids = jnp.stack([lax.axis_index("tile"), lax.axis_index("mem")]).astype(jnp.int32)
        whole = lambda a: pl.BlockSpec(a.shape, lambda *_: (0,) * a.ndim)

        def pert_spec(offset, row=0):
            return pl.BlockSpec(
                (base, levels, ROWS, columns), lambda x, m, _: (offset + m, 0, row + x, 0)
            )

        order = partners(tiles)

        def exchange(pieces):
            moved = list(pieces)
            for i in range(1, tiles):
                pairs = [(k, k ^ order[i]) for k in range(tiles)]
                moved[i] = lax.ppermute(pieces[i], "tile", pairs)
            return moved

        def restrict(offset, steps, row, part, grant):
            width = steps * base
            row = row // ROWS
            units = width * modes * lane_blocks // tiles
            piece = jax.ShapeDtypeStruct((units, part, LANES), jnp.bfloat16)
            pixels = width * part
            return call(
                lambda *refs: restrict_kernel(tiles, width, *refs),
                flops=2 * pixels * levels * MY * (columns + modes * HALF),
                moved=2 * pixels * levels * columns + 4 * levels * part * columns,
                grant=grant,
                out_shape=[piece] * tiles,
                grid_spec=pltpu.PrefetchScalarGridSpec(
                    num_scalar_prefetch=1,
                    grid=(part // ROWS, steps),
                    in_specs=[
                        pert_spec(offset, row),
                        pl.BlockSpec((levels, ROWS, columns), lambda x, m, _: (0, row + x, 0)),
                        whole(y_in),
                        whole(z_in),
                    ],
                    out_specs=[pl.BlockSpec((units, ROWS, LANES), lambda x, m, _: (0, x, 0))]
                    * tiles,
                    scratch_shapes=[pltpu.VMEM((units * tiles, ROWS, LANES), jnp.bfloat16)],
                ),
            )(ids, perturbations, increment, y_in, z_in)

        def localize(sets, steps, parts):
            width = steps * base
            pieces = [p for pieces in sets for p in pieces]
            units = pieces[0].shape[0]
            group = next(g for g in (3, 2, 1) if units % g == 0)
            spec = lambda rows: pl.BlockSpec((group, rows, LANES), lambda i, _: (i, 0, 0))

            def matrix_spec(g):
                def index(i, ids):
                    return ((ids[0] * units + i * group + g) // (width * lane_blocks), 0, 0)

                return pl.BlockSpec((1, modes_x, modes_x), index)

            cells = height * tiles
            wide = group * LANES
            heights = [rows for rows in parts for _ in range(tiles)]
            outs = call(
                lambda *refs: localize_kernel(tiles, group, len(sets), *refs),
                flops=2 * units * LANES * modes_x * (2 * cells + modes_x),
                moved=units * (4 * LANES * cells + 2 * modes_x * modes_x),
                out_shape=[
                    jax.ShapeDtypeStruct((units, rows, LANES), jnp.bfloat16) for rows in heights
                ],
                grid_spec=pltpu.PrefetchScalarGridSpec(
                    num_scalar_prefetch=1,
                    grid=(units // group,),
                    in_specs=[spec(p.shape[1]) for p in pieces]
                    + [matrix_spec(g) for g in range(group)]
                    + [whole(x_in), whole(x_out)],
                    out_specs=[spec(rows) for rows in heights],
                    scratch_shapes=[
                        pltpu.VMEM((cells, wide), jnp.bfloat16),
                        pltpu.VMEM((cells, wide), jnp.bfloat16),
                    ],
                ),
            )(ids, *pieces, *([localization] * group), x_in, x_out)
            return [outs[i * tiles : (i + 1) * tiles] for i in range(len(parts))]

        def prolong(pieces, before, offset, steps, final, row=0):
            width = steps * base
            units, part, _ = pieces[0].shape
            row = row // ROWS
            full = jax.ShapeDtypeStruct((levels, part, columns), jnp.float32)
            half = jax.ShapeDtypeStruct((levels, part, columns // 2), jnp.float32)
            block = lambda n, r=0: pl.BlockSpec((levels, ROWS, n), lambda x, m, _: (0, r + x, 0))
            start = before is None
            pixels = width * part
            return call(
                lambda *refs: prolong_kernel(tiles, width, start, final, *refs),
                flops=2 * pixels * levels * MY * (columns + modes * HALF),
                moved=2 * pixels * levels * columns + 8 * levels * part * columns,
                out_shape=[half, half] if final else [full],
                grid_spec=pltpu.PrefetchScalarGridSpec(
                    num_scalar_prefetch=1,
                    grid=(part // ROWS, steps),
                    in_specs=[pert_spec(offset, row), whole(y_out), whole(z_out)]
                    + [pl.BlockSpec((units, ROWS, LANES), lambda x, m, _: (0, x, 0))] * tiles
                    + ([] if start else [block(columns, row)]),
                    out_specs=[block(columns // 2)] * 2 if final else [block(columns)],
                    scratch_shapes=[
                        pltpu.VMEM((units * tiles, ROWS, LANES), jnp.bfloat16),
                        pltpu.VMEM((levels, ROWS, columns), jnp.float32),
                    ],
                ),
            )(ids, perturbations, y_out, z_out, *pieces, *([] if start else [before]))

        def finish(own, received, before, row):
            part = own.shape[1]
            depth = levels // 2 if levels % 2 == 0 else levels
            spec = pl.BlockSpec((depth, part, columns // 2), lambda z: (z, 0, 0))
            where = pl.BlockSpec(
                (pl.Element(depth), pl.Element(part), pl.Element(columns // 2)),
                lambda z: (z * depth, row, 0),
            )
            return call(
                finish_kernel,
                flops=own.size,
                moved=12 * own.size,
                out_shape=jax.ShapeDtypeStruct((levels, height, columns // 2), jnp.float32),
                grid=(levels // depth,),
                in_specs=[spec, spec]
                + ([] if before is None else [pl.BlockSpec(memory_space=pl.ANY)]),
                out_specs=where,
                input_output_aliases={} if before is None else {2: 0},
            )(own, received, *([] if before is None else [before]))

        offsets = [sum(plan[:i]) for i in range(len(plan))]
        last = len(plan) - 1
        arrived = []
        for i, n in enumerate(plan):
            sets, row = [], 0
            for part in heads if i == 0 else [height]:
                made = restrict(offsets[i], n, row, part, 62 if i < 2 else 30)
                sets.append(exchange(made))
                row += part
            arrived.append(sets)
        returned = []
        for i, n in enumerate(plan):
            parts = localize(arrived[i], n, tails if i == last else [height])
            returned.append([exchange(p) for p in parts])
        total = None
        for i in range(last):
            (total,) = prolong(returned[i][0], total, offsets[i], plan[i], False)
        sums, starts = [], []
        for pieces in returned[last]:
            starts.append(sum(tails[: len(starts)]))
            sums.append(prolong(pieces, total, offsets[last], plan[last], True, starts[-1]))
        received = [lax.ppermute(other, "mem", [(0, 1), (1, 0)]) for _, other in sums]
        result = None
        for (own, _), other, row in zip(sums, received, starts):
            result = finish(own, other, result, row)
        return result

    def run(increment, perturbations, localization):
        members = perturbations.shape[0] // mesh.shape["mem"]
        modes, height = localization.shape[0], increment.shape[1] // tiles
        units = modes * (MY // LANES)
        base, plan = chunk_plan(members, units, tiles)
        half = height // 2 // ROWS * ROWS
        heads = [height]
        tails = [half, height - half] if half else [height]
        step = jax.shard_map(
            functools.partial(shards, base=base, plan=plan, heads=heads, tails=tails),
            mesh=mesh,
            in_specs=(P("grp", "tile", None), P("mem", "grp", "tile", None), P()),
            out_specs=P("grp", "tile", "mem"),
            check_vma=False,
        )
        return step(increment, perturbations, localization)

    return run
```

```python
import functools
import math

import jax
import jax.numpy as jnp
import numpy as np
from jax import lax
from jax.experimental import pallas as pl
from jax.experimental.pallas import tpu as pltpu
from jax.sharding import PartitionSpec as P


MY = 256
LANES = 128
ROWS = 16
HALF = 8


def make_table(modes, cells):
    index = np.arange(modes, dtype=np.float32)[:, None]
    points = np.arange(cells, dtype=np.float32)[None, :]
    weights = np.where(index == 0, math.sqrt(1.0 / cells), math.sqrt(2.0 / cells))
    angles = np.float32(math.pi) * index * (2.0 * points + 1.0) / np.float32(2.0 * cells)
    return (weights.astype(np.float32) * np.cos(angles)).astype(jnp.bfloat16)


def partners(tiles):
    order = [0]
    for s in range(tiles // 2):
        order += [tiles // 2 + (s ^ (s >> 1)), s + 1]
    return order[:tiles]


def dot(a, b):
    return jnp.dot(a, b, preferred_element_type=jnp.float32)


def restrict_kernel(tiles, width, ids, pert, inc, table, vertical, *rest):
    outs, stage = rest[:tiles], rest[tiles]
    count, levels = pert.shape[0], pert.shape[1]
    halves = ROWS // HALF
    modes = vertical.shape[0] // HALF
    lane_blocks = table.shape[1] // LANES
    first = pl.program_id(1) * count
    field = inc[...]
    for m in range(count):
        product = (pert[m].astype(jnp.float32) * field).astype(jnp.bfloat16)
        along_y = dot(product.reshape(levels * ROWS, -1), table[...])
        along_y = along_y.reshape(levels, halves, HALF, -1)
        parts = []
        for h in range(halves):
            part = along_y[:, h].reshape(levels * HALF, -1).astype(jnp.bfloat16)
            parts.append(dot(vertical[...], part).reshape(modes, HALF, -1))
        along_z = jnp.concatenate(parts, axis=1).astype(jnp.bfloat16)
        for c in range(modes):
            for q in range(lane_blocks):
                stage[(c * width + first + m) * lane_blocks + q] = along_z[
                    c, :, q * LANES : (q + 1) * LANES
                ]

    @pl.when(pl.program_id(1) == pl.num_programs(1) - 1)
    def _():
        units = outs[0].shape[0]
        for out, s in zip(outs, partners(tiles)):
            out[...] = stage[pl.ds(jnp.bitwise_xor(ids[0], s) * units, units)]


def localize_kernel(tiles, group, cuts, ids, *rest):
    pieces, rest = rest[: tiles * cuts], rest[tiles * cuts :]
    matrices, rest = rest[:group], rest[group:]
    table, table_t = rest[:2]
    outs, (field, prolonged) = rest[2:-2], rest[-2:]
    height = field.shape[0] // tiles
    order = partners(tiles)

    def places(refs):
        start = 0
        for i, ref in enumerate(refs):
            base = jnp.bitwise_xor(ids[0], order[i % tiles]) * height + start
            yield ref, pl.ds(pl.multiple_of(base, ROWS), ref.shape[1])
            start += ref.shape[1] if i % tiles == tiles - 1 else 0

    for piece, rows in places(pieces):
        for g in range(group):
            field[rows, g * LANES : (g + 1) * LANES] = piece[g]
    spectral = dot(table[...], field[...]).astype(jnp.bfloat16)
    localized = [
        dot(matrices[g][0], spectral[:, g * LANES : (g + 1) * LANES]).astype(jnp.bfloat16)
        for g in range(group)
    ]
    prolonged[...] = dot(table_t[...], jnp.concatenate(localized, axis=1)).astype(jnp.bfloat16)
    for out, rows in places(outs):
        for g in range(group):
            out[g] = prolonged[rows, g * LANES : (g + 1) * LANES]


def prolong_kernel(tiles, width, start, final, ids, pert, table, vertical, *rest):
    pieces, rest = rest[:tiles], rest[tiles:]
    before, rest = (None, rest) if start else (rest[0], rest[1:])
    if width == pert.shape[0]:
        outs, stage, total = rest[:-1], rest[-1], None
    else:
        outs, stage, total = rest[:-2], rest[-2], rest[-1]
    count, levels = pert.shape[0], pert.shape[1]
    halves = ROWS // HALF
    modes = vertical.shape[1] // HALF
    lane_blocks = table.shape[0] // LANES
    first = pl.program_id(1) * count

    def store(value):
        for h in range(halves):
            rows = slice(h * HALF, (h + 1) * HALF)
            if final:
                own, other = outs
                half = own.shape[2]
                low, high = value(h)[..., :half], value(h)[..., half:]
                own[:, rows] = jnp.where(ids[1] == 0, low, high)
                other[:, rows] = jnp.where(ids[1] == 0, high, low)
            else:
                outs[0][:, rows] = value(h)

    @pl.when(pl.program_id(1) == 0)
    def _():
        units = pieces[0].shape[0]
        for piece, s in zip(pieces, partners(tiles)):
            stage[pl.ds(jnp.bitwise_xor(ids[0], s) * units, units)] = piece[...]

    if total is not None:

        @pl.when(pl.program_id(1) == 0)
        def _():
            total[...] = jnp.zeros_like(total) if start else before[...]

    sums = [None] * halves
    for m in range(count):
        rows = []
        for c in range(modes):
            unit = (c * width + first + m) * lane_blocks
            rows.append(
                jnp.concatenate([stage[unit + q] for q in range(lane_blocks)], axis=1)
            )
        back_x = jnp.stack(rows).astype(jnp.float32).reshape(modes, halves, HALF, -1)
        for h in range(halves):
            part = back_x[:, h].reshape(modes * HALF, -1).astype(jnp.bfloat16)
            back_z = dot(vertical[...], part).astype(jnp.bfloat16)
            back_y = dot(back_z, table[...]).reshape(levels, HALF, -1)
            term = pert[m].astype(jnp.float32)[:, h * HALF : (h + 1) * HALF] * back_y
            sums[h] = term if sums[h] is None else sums[h] + term

    if total is not None:
        for h in range(halves):
            total[:, h * HALF : (h + 1) * HALF] += sums[h]

        @pl.when(pl.program_id(1) == pl.num_programs(1) - 1)
        def _():
            store(lambda h: total[:, h * HALF : (h + 1) * HALF])

    else:

        def value(h):
            return sums[h] if start else before[:, h * HALF : (h + 1) * HALF] + sums[h]

        store(value)


def finish_kernel(*refs):
    own, received, out = refs[0], refs[1], refs[-1]
    out[...] = own[...] + received[...]


def chunk_plan(members, units_per_member, tiles):
    base = next(
        b
        for b in range(1, members + 1)
        if members % b == 0 and (b * units_per_member) % tiles == 0
    )
    left = members // base
    plan = []
    if left >= 5:
        plan, left = [1, 1], left - 4
        while left >= 2:
            plan, left = plan + [2], left - 2
        plan = plan + [1] * left + [1, 1]
    else:
        plan = [1] * left
    return base, plan


def solution(mesh):
    tiles = mesh.shape["tile"]

    def call(kernel, flops, moved, grant=30, **kwargs):
        return pl.pallas_call(
            kernel,
            compiler_params=pltpu.CompilerParams(vmem_limit_bytes=grant * 1024 * 1024),
            cost_estimate=pl.CostEstimate(
                flops=int(flops), bytes_accessed=int(moved), transcendentals=0
            ),
            **kwargs,
        )

    def shards(increment, perturbations, localization, base, plan, heads, tails):
        _, levels, height, columns = perturbations.shape
        modes, modes_x, _ = localization.shape
        lane_blocks = MY // LANES
        table_y = make_table(MY, columns)
        table_x = make_table(modes_x, height * tiles)
        table_z = make_table(modes, levels)
        eye = np.eye(HALF, dtype=np.float32)
        vertical = np.kron(table_z.astype(np.float32), eye).astype(jnp.bfloat16)
        y_in, y_out = jnp.asarray(table_y.T), jnp.asarray(table_y)
        x_in, x_out = jnp.asarray(table_x), jnp.asarray(table_x.T)
        z_in, z_out = jnp.asarray(vertical), jnp.asarray(vertical.T)
        ids = jnp.stack([lax.axis_index("tile"), lax.axis_index("mem")]).astype(jnp.int32)
        whole = lambda a: pl.BlockSpec(a.shape, lambda *_: (0,) * a.ndim)

        def pert_spec(offset, row=0):
            return pl.BlockSpec(
                (base, levels, ROWS, columns), lambda x, m, _: (offset + m, 0, row + x, 0)
            )

        order = partners(tiles)

        def exchange(pieces):
            moved = list(pieces)
            for i in range(1, tiles):
                pairs = [(k, k ^ order[i]) for k in range(tiles)]
                moved[i] = lax.ppermute(pieces[i], "tile", pairs)
            return moved

        def restrict(offset, steps, row, part, grant):
            width = steps * base
            row = row // ROWS
            units = width * modes * lane_blocks // tiles
            piece = jax.ShapeDtypeStruct((units, part, LANES), jnp.bfloat16)
            pixels = width * part
            return call(
                lambda *refs: restrict_kernel(tiles, width, *refs),
                flops=2 * pixels * levels * MY * (columns + modes * HALF),
                moved=2 * pixels * levels * columns + 4 * levels * part * columns,
                grant=grant,
                out_shape=[piece] * tiles,
                grid_spec=pltpu.PrefetchScalarGridSpec(
                    num_scalar_prefetch=1,
                    grid=(part // ROWS, steps),
                    in_specs=[
                        pert_spec(offset, row),
                        pl.BlockSpec((levels, ROWS, columns), lambda x, m, _: (0, row + x, 0)),
                        whole(y_in),
                        whole(z_in),
                    ],
                    out_specs=[pl.BlockSpec((units, ROWS, LANES), lambda x, m, _: (0, x, 0))]
                    * tiles,
                    scratch_shapes=[pltpu.VMEM((units * tiles, ROWS, LANES), jnp.bfloat16)],
                ),
            )(ids, perturbations, increment, y_in, z_in)

        def localize(sets, steps, parts):
            width = steps * base
            pieces = [p for pieces in sets for p in pieces]
            units = pieces[0].shape[0]
            group = next(g for g in (3, 2, 1) if units % g == 0)
            spec = lambda rows: pl.BlockSpec((group, rows, LANES), lambda i, _: (i, 0, 0))

            def matrix_spec(g):
                def index(i, ids):
                    return ((ids[0] * units + i * group + g) // (width * lane_blocks), 0, 0)

                return pl.BlockSpec((1, modes_x, modes_x), index)

            cells = height * tiles
            wide = group * LANES
            heights = [rows for rows in parts for _ in range(tiles)]
            outs = call(
                lambda *refs: localize_kernel(tiles, group, len(sets), *refs),
                flops=2 * units * LANES * modes_x * (2 * cells + modes_x),
                moved=units * (4 * LANES * cells + 2 * modes_x * modes_x),
                out_shape=[
                    jax.ShapeDtypeStruct((units, rows, LANES), jnp.bfloat16) for rows in heights
                ],
                grid_spec=pltpu.PrefetchScalarGridSpec(
                    num_scalar_prefetch=1,
                    grid=(units // group,),
                    in_specs=[spec(p.shape[1]) for p in pieces]
                    + [matrix_spec(g) for g in range(group)]
                    + [whole(x_in), whole(x_out)],
                    out_specs=[spec(rows) for rows in heights],
                    scratch_shapes=[
                        pltpu.VMEM((cells, wide), jnp.bfloat16),
                        pltpu.VMEM((cells, wide), jnp.bfloat16),
                    ],
                ),
            )(ids, *pieces, *([localization] * group), x_in, x_out)
            return [outs[i * tiles : (i + 1) * tiles] for i in range(len(parts))]

        def prolong(pieces, before, offset, steps, final, row=0):
            width = steps * base
            units, part, _ = pieces[0].shape
            row = row // ROWS
            full = jax.ShapeDtypeStruct((levels, part, columns), jnp.float32)
            half = jax.ShapeDtypeStruct((levels, part, columns // 2), jnp.float32)
            block = lambda n, r=0: pl.BlockSpec((levels, ROWS, n), lambda x, m, _: (0, r + x, 0))
            start = before is None
            pixels = width * part
            return call(
                lambda *refs: prolong_kernel(tiles, width, start, final, *refs),
                flops=2 * pixels * levels * MY * (columns + modes * HALF),
                moved=2 * pixels * levels * columns + 8 * levels * part * columns,
                out_shape=[half, half] if final else [full],
                grid_spec=pltpu.PrefetchScalarGridSpec(
                    num_scalar_prefetch=1,
                    grid=(part // ROWS, steps),
                    in_specs=[pert_spec(offset, row), whole(y_out), whole(z_out)]
                    + [pl.BlockSpec((units, ROWS, LANES), lambda x, m, _: (0, x, 0))] * tiles
                    + ([] if start else [block(columns, row)]),
                    out_specs=[block(columns // 2)] * 2 if final else [block(columns)],
                    scratch_shapes=[
                        pltpu.VMEM((units * tiles, ROWS, LANES), jnp.bfloat16),
                        *([pltpu.VMEM((levels, ROWS, columns), jnp.float32)] if steps > 1 else []),
                    ],
                ),
            )(ids, perturbations, y_out, z_out, *pieces, *([] if start else [before]))

        def finish(own, received, before, row):
            part = own.shape[1]
            depth = levels // 2 if levels % 2 == 0 else levels
            spec = pl.BlockSpec((depth, part, columns // 2), lambda z: (z, 0, 0))
            where = pl.BlockSpec(
                (pl.Element(depth), pl.Element(part), pl.Element(columns // 2)),
                lambda z: (z * depth, row, 0),
            )
            return call(
                finish_kernel,
                flops=own.size,
                moved=12 * own.size,
                out_shape=jax.ShapeDtypeStruct((levels, height, columns // 2), jnp.float32),
                grid=(levels // depth,),
                in_specs=[spec, spec]
                + ([] if before is None else [pl.BlockSpec(memory_space=pl.ANY)]),
                out_specs=where,
                input_output_aliases={} if before is None else {2: 0},
            )(own, received, *([] if before is None else [before]))

        offsets = [sum(plan[:i]) for i in range(len(plan))]
        last = len(plan) - 1
        arrived = []
        for i, n in enumerate(plan):
            sets, row = [], 0
            for part in heads if i == 0 else [height]:
                made = restrict(offsets[i], n, row, part, 62 if i < 2 else 30)
                sets.append(exchange(made))
                row += part
            arrived.append(sets)
        returned = []
        for i, n in enumerate(plan):
            parts = localize(arrived[i], n, tails if i == last else [height])
            returned.append([exchange(p) for p in parts])
        total = None
        for i in range(last):
            (total,) = prolong(returned[i][0], total, offsets[i], plan[i], False)
        sums, starts = [], []
        for pieces in returned[last]:
            starts.append(sum(tails[: len(starts)]))
            sums.append(prolong(pieces, total, offsets[last], plan[last], True, starts[-1]))
        received = [lax.ppermute(other, "mem", [(0, 1), (1, 0)]) for _, other in sums]
        result = None
        for (own, _), other, row in zip(sums, received, starts):
            result = finish(own, other, result, row)
        return result

    def run(increment, perturbations, localization):
        members = perturbations.shape[0] // mesh.shape["mem"]
        modes, height = localization.shape[0], increment.shape[1] // tiles
        units = modes * (MY // LANES)
        base, plan = chunk_plan(members, units, tiles)
        half = height // 2 // ROWS * ROWS
        heads = [half, height - half] if half else [height]
        tails = [half, height - half] if half else [height]
        step = jax.shard_map(
            functools.partial(shards, base=base, plan=plan, heads=heads, tails=tails),
            mesh=mesh,
            in_specs=(P("grp", "tile", None), P("mem", "grp", "tile", None), P()),
            out_specs=P("grp", "tile", "mem"),
            check_vma=False,
        )
        return step(increment, perturbations, localization)

    return run
```
